1024 devices in a mesh: vir: 128 (over x, z_lo, y), ph: 4 (over z_hi), vec: 2 (over core).
Axes of the slice: x: 8, y: 8, z: 8 (z_hi: 4, z_lo: 2; z = z_hi * 2 + z_lo), core: 2. Of those that a mesh axis runs over, the one named last changes fastest.
Arguments:
- vv_factor: bfloat16 [1024, 1024, 1024], P(('ph', 'vec'), 'vir'), may hold values from -0.1875 to 0.1875
- ladder_amp: bfloat16 [1024, 1024, 256], P(None, 'vir'), may hold values from -0.1875 to 0.1875
- cycle_amp: bfloat16 [1024, 32, 128], P(('vir', 'ph'), None, 'vec'), may hold values from -0.015625 to 0.015625
- ov_slots: bfloat16 [2048, 1024, 128], P(('vir', 'ph'), None, 'vec'), may hold values from -6 to 6
- owner_of: int32 [1024], P(('vir', 'ph')), may hold values from 0 to 3, as said below
- slot_of: int32 [1024], P(('vir', 'ph')), may hold values from 0 to 3, as said below
- ov_pairs: bfloat16 [1024, 8, 1024], P(('ph', 'vec'), None, 'vir'), may hold values from -0.1875 to 0.1875
- eps_vir: float32 [1024], replicated, may hold values from 0.5 to 3
- eps_occ: float32 [128], replicated, may hold values from -3 to -0.5
Outputs:
- residual: bfloat16 [1024, 256], P('vir', ('ph', 'vec'))
- update: float32 [1024, 256], P('vir', ('ph', 'vec'))
The draws below stay inside these ranges and needn't reach their ends.
Inputs may be any that keep to these rules, and one draw needn't show every extreme that they name: `owner_of`: within each run of 8 consecutive blocks (one vir index) one owner holds exactly 4 blocks and no owner more. `slot_of`: distinct among the blocks of one run with the same owner.
All inputs are finite; a program needn't handle non-finite values.
Results may differ from the reference program's by a relative error of at most 0.0055.
Values may be sent and summed in bfloat16 or wider, within the bound.
A program may use at most 64 MiB of HBM per device.

```python
import jax
import jax.numpy as jnp
from jax import lax

V = 1024
NCHOL = 1024
NOCC = 128
BW = 128
I_OCC = 32
J_OCC = 8
NPAIR = 256
NBLK = 1024
NBD = 2
CAPB = 4
N_VIR = 128
N_PH = 4


def cycle_layout(key):
    group_size = N_PH * NBD

    def layout_group(group_index):
        subkey = jax.random.fold_in(key, group_index)
        first_key, second_key, third_key, fourth_key = jax.random.split(subkey, 4)
        shuffle = jax.random.permutation(first_key, group_size)
        busiest = jax.random.randint(second_key, (), 0, N_PH)
        offset = jax.random.randint(third_key, (), 0, N_PH - 1)
        position = jnp.arange(group_size)
        spread = (position - CAPB + offset) % (N_PH - 1)
        spread = spread + (spread >= busiest).astype(spread.dtype)
        by_position = jnp.where(position < CAPB, busiest, spread)
        owners = jnp.zeros((group_size,), by_position.dtype).at[shuffle].set(by_position)
        matches = (owners[:, None] == jnp.arange(N_PH)[None, :]).astype(owners.dtype)
        ranking = jnp.cumsum(matches, 0) - matches
        ranks = jnp.sum(ranking * matches, 1)
        owner_keys = jax.random.split(fourth_key, N_PH)
        orders = jax.vmap(lambda k: jax.random.permutation(k, CAPB))(owner_keys)
        slots = orders[owners, ranks]
        return (owners, slots)
    owners, slots = jax.vmap(layout_group)(jnp.arange(N_VIR))
    return (owners.reshape(-1).astype(jnp.int32), slots.reshape(-1).astype(jnp.int32))


def draw_owner_of(key, part):
    return cycle_layout(jax.random.fold_in(key, 11))[0]


def draw_slot_of(key, part):
    return cycle_layout(jax.random.fold_in(key, 11))[1]


def block_levels(rng, extent, cuts, low, largest):
    def one(dim, blocks):
        draws = jax.random.uniform(jax.random.fold_in(jax.random.fold_in(rng, 6), dim), (blocks,), jnp.float32, low / len(cuts), largest / len(cuts))
        return jnp.repeat(jnp.exp(draws), extent[dim] // blocks).reshape((-1,) + (1,) * (len(extent) - dim - 1))

    level = one(*cuts[0])
    for cut in cuts[1:]:
        level = level * one(*cut)
    return level


def scatter_about(key, dims, scale, bound, cuts=(), kind=jnp.bfloat16):
    values = scale * jax.random.normal(key, dims, jnp.float32)
    if cuts:
        values = values * block_levels(key, dims, cuts, -0.22, 0.18)
    return jnp.clip(values, -bound, bound).astype(kind)


def setup_inputs(seed: int = 0) -> dict:
    splits = jax.random.split(jax.random.key(seed), 10)
    return {
        "vv_factor": scatter_about(splits[0], (NCHOL, V, V), V ** -0.5, 0.1875, ((0, 8), (1, 128))),
        "ladder_amp": scatter_about(splits[1], (V, V, NPAIR), NCHOL ** -0.5, 0.1875, ((1, 128),)),
        "cycle_amp": scatter_about(splits[2], (NBLK, I_OCC, BW), (NOCC * V) ** -0.5, 0.015625, ((0, 512), (2, 2))),
        "ov_slots": scatter_about(splits[3], (N_VIR * N_PH * CAPB, NCHOL, BW), 1.0, 6.0, ((0, 512), (2, 2))),
        "owner_of": draw_owner_of(jax.random.fold_in(splits[9], 71), 0),
        "slot_of": draw_slot_of(jax.random.fold_in(splits[9], 71), 0),
        "ov_pairs": scatter_about(splits[6], (NCHOL, J_OCC, V), NCHOL ** -0.5, 0.1875, ((0, 8), (2, 128))),
        "eps_vir": jnp.clip(jax.random.uniform(splits[7], (V,), jnp.float32, 0.5, 3.0), 0.5, 3.0),
        "eps_occ": jnp.clip(jax.random.uniform(splits[8], (NOCC,), jnp.float32, -3.0, -0.5), -3.0, -0.5),
    }


def reference(vv_factor, ladder_amp, cycle_amp, ov_slots, owner_of, slot_of, ov_pairs, eps_vir, eps_occ):
    factor_row = vv_factor[:, :, 0]
    amp_matrix = ladder_amp.reshape(V, V * NPAIR)
    block_count = 8
    block_size = NCHOL // block_count

    def ladder_block(carry, block_index):
        start = (block_index * block_size).astype(jnp.int32)
        rows_part = lax.dynamic_slice_in_dim(factor_row, start, block_size, 0)
        half = jnp.dot(rows_part, amp_matrix, preferred_element_type=jnp.float32).astype(jnp.bfloat16)
        half = half.reshape(block_size * V, NPAIR)
        factor_block = lax.dynamic_slice_in_dim(vv_factor, start, block_size, 0).reshape(block_size * V, V)
        term = lax.dot_general(factor_block, half, (((0,), (0,)), ((), ())), preferred_element_type=jnp.float32)
        return carry + term, None

    ladder, unused = lax.scan(ladder_block, jnp.zeros((V, NPAIR), jnp.float32), jnp.arange(block_count, dtype=jnp.int32))

    group_size = N_PH * NBD
    group_of = jnp.arange(NBLK, dtype=jnp.int32) // group_size
    slot_rows = ((group_of * N_PH + owner_of) * CAPB + slot_of).astype(jnp.int32)

    def cycle_group(carry, inputs):
        amps, row_ids = inputs
        picked = jnp.take(ov_slots, row_ids, axis=0).astype(jnp.float32)
        return carry + jnp.einsum("giw,gpw->ip", amps.astype(jnp.float32), picked), None

    coupling, unused_too = lax.scan(
        cycle_group,
        jnp.zeros((I_OCC, NCHOL), jnp.float32),
        (cycle_amp.reshape(N_VIR, group_size, I_OCC, BW), slot_rows.reshape(N_VIR, group_size)),
    )
    coupling = coupling.astype(jnp.bfloat16)
    cycle = jnp.einsum("ip,pjb->bij", coupling.astype(jnp.float32), ov_pairs.astype(jnp.float32)).reshape(V, NPAIR)
    residual = (ladder + cycle).astype(jnp.bfloat16)
    pair_index = jnp.arange(NPAIR, dtype=jnp.int32)
    first_occ = eps_occ[pair_index // J_OCC]
    second_occ = eps_occ[pair_index % J_OCC]
    denominator = (eps_vir[0] + eps_vir)[:, None] - first_occ[None, :] - second_occ[None, :]
    update = residual.astype(jnp.float32) / denominator
    return residual, update
```

```python
import functools

import jax
import jax.numpy as jnp
from jax import lax
from jax.experimental import pallas as pl
from jax.experimental.pallas import tpu as pltpu
from jax.sharding import Mesh
from jax.sharding import PartitionSpec as P

AXES = ("vir_0", "vir_1", "vir_2", "ph", "vec")
VIR = ("vir_0", "vir_1", "vir_2")
VIR_PH = ("vir_0", "vir_1", "vir_2", "ph")
F32 = jnp.float32
BF16 = jnp.bfloat16
R = 8
LANES = 128


def far_first(count):
    return sorted(range(1, count), key=lambda d: -min(d, count - d))


def body(
    sizes,
    factor,
    amp,
    cycle_amp,
    ov_slots,
    owner_of,
    slot_of,
    ov_pairs,
    eps_vir,
    eps_occ,
    residual_ref,
    update_ref,
    factor_raw,
    factor_wide,
    factor_t,
    amp_raw,
    amp_wide,
    amp_d,
    rows,
    row_lhs,
    half,
    slots_v,
    cyc_v,
    pairs_v,
    blk_send,
    blk_recv,
    part,
    part_recv,
    c1,
    c1_recv,
    c2,
    c2_recv,
    c3,
    c3_recv,
    cyc,
    cyc_recv,
    grid,
    grid_recv,
    wide,
    stage,
    stage_recv,
    second,
    second_recv,
    third,
    third_recv,
    load_sem,
    send_sem,
    recv_sem,
):
    nx, nl, ny, nh, nk = sizes
    pc = factor.shape[0]
    pairs = amp.shape[2]
    slab = nl * ny * R
    part_rows = ny * R
    x, l, y, h, k = (lax.axis_index(a) for a in AXES)
    me = {"vir_0": x, "vir_1": l, "vir_2": y, "ph": h, "vec": k}

    def at(**moved):
        return tuple(moved.get(a, me[a]) for a in AXES)

    def step(axis, value, d, count):
        return {axis: lax.rem(value + d, count)}

    ids = iter(range(1000))

    def remote(src, dst, target, slot):
        return pltpu.make_async_remote_copy(
            src_ref=src,
            dst_ref=dst,
            send_sem=send_sem.at[slot],
            recv_sem=recv_sem.at[slot],
            device_id=target,
            device_id_type=pl.DeviceIdType.MESH,
        )

    sent = []

    def start(copies):
        for c in copies:
            c.start()
        sent.extend(copies)

    def arrive(copies):
        for c in copies:
            c.wait_recv()

    x_steps, y_steps = far_first(nx), far_first(ny)
    z_steps = [(dh, dk) for dh in range(nh) for dk in range(nk) if dh or dk]

    barrier = pltpu.get_barrier_semaphore()
    partners = [step("vir_0", x, d, nx) for d in x_steps]
    partners += [step("vir_2", y, d, ny) for d in y_steps]
    partners += [
        {**step("ph", h, dh, nh), **step("vec", k, dk, nk), **step("vir_1", l, dl, nl)}
        for dl in range(nl)
        for dh in range(nh)
        for dk in range(nk)
        if dl or dh or dk
    ]
    for moved in partners:
        pl.semaphore_signal(
            barrier, inc=1, device_id=at(**moved), device_id_type=pl.DeviceIdType.MESH
        )

    loads = []

    def load(src, dst):
        copy = pltpu.make_async_copy(src, dst, load_sem.at[len(loads)])
        copy.start()
        loads.append(copy)
        return copy

    factor_loads = [
        load(factor.at[:, :, pl.ds(s * slab, slab)], factor_raw.at[s]) for s in range(nx)
    ]
    cyc_load = load(cycle_amp, cyc_v)
    slots_load = load(ov_slots, slots_v)
    amp_loads = [
        load(amp.at[pl.ds(s * slab, slab)], amp_raw.at[pl.ds(s * slab, slab)]) for s in range(nx)
    ]
    pairs_load = load(ov_pairs, pairs_v)

    cyc_load.wait()
    blocks = [jnp.concatenate([cyc_v[n].astype(F32)] * 2, axis=1) for n in range(2)]
    lane_half = (
        lax.broadcasted_iota(jnp.int32, blocks[0].shape, 1) >= blocks[0].shape[1] // 2
    ).astype(jnp.int32)
    for target in range(nh):
        for pair in range(2):
            total = jnp.zeros_like(blocks[0])
            for n in range(2):
                wanted = jnp.where(owner_of[n] == target, slot_of[n], -1)
                total = total + jnp.where(lane_half + 2 * pair == wanted, blocks[n], 0.0)
            blk_send[target, pair] = total.astype(BF16)

    factor_loads[0].wait()
    first = factor_raw[0].astype(F32)[:, :, :1]
    lane_of = lax.broadcasted_iota(jnp.int32, (pc, R, pc), 2)
    row_of = lax.broadcasted_iota(jnp.int32, (pc, R, pc), 0)
    piece = jnp.sum(jnp.where(lane_of == row_of, first, 0.0), axis=0).astype(BF16)
    outer = jnp.where(l == 0, y, x)
    inner = jnp.where(l == 0, x, y)
    rows[l, outer, inner] = piece

    pl.semaphore_wait(barrier, len(partners))

    pick = rows.at[l, outer, inner]
    gather0 = [remote(pick, pick, at(**step("vir_1", l, 1, nl)), next(ids))]
    start(gather0)
    to_owner = []
    for d in far_first(nh):
        moved = step("ph", h, d, nh)
        to_owner.append(
            remote(blk_send.at[moved["ph"]], blk_recv.at[d - 1], at(**moved), next(ids))
        )
    start(to_owner)

    arrive(gather0)
    gather1 = []
    for dx, dy in zip(x_steps, y_steps):
        own0, own1 = rows.at[0, y, x], rows.at[1, x, y]
        gather1.append(remote(own0, own0, at(**step("vir_0", x, dx, nx)), next(ids)))
        gather1.append(remote(own1, own1, at(**step("vir_2", y, dy, ny)), next(ids)))
    start(gather1)

    for copy in factor_loads[1:]:
        copy.wait()

    def turn_factor(s, carry):
        factor_wide[...] = factor_raw[s].astype(F32).reshape(factor_wide.shape)
        base = pl.multiple_of(s * part_rows, part_rows)
        for d in range(R):
            turned = factor_wide[pl.ds(d, pc, stride=R), :].T.astype(BF16)
            for c in range(nl):
                factor_t[c, pl.ds(base, part_rows), d * pc : (d + 1) * pc] = turned[
                    c * part_rows : (c + 1) * part_rows
                ]
        return carry

    lax.fori_loop(0, nx, turn_factor, 0)

    slots_load.wait()
    arrive(to_owner)
    arranged = blk_send[h].astype(F32)
    for d in range(nh - 1):
        arranged = arranged + blk_recv[d].astype(F32)
    arranged = arranged.astype(BF16)
    depth = slots_v.shape[0] // 2
    for q in range(nh * nk):
        chunk = slice(q * pc, (q + 1) * pc)
        part[q] = jnp.dot(
            arranged[0], slots_v[:depth, chunk], preferred_element_type=F32
        ) + jnp.dot(arranged[1], slots_v[depth:, chunk], preferred_element_type=F32)
    to_chunk = []
    for n, (dh, dk) in enumerate(z_steps):
        moved = {**step("ph", h, dh, nh), **step("vec", k, dk, nk)}
        to_chunk.append(
            remote(
                part.at[moved["ph"] * nk + moved["vec"]], part_recv.at[n], at(**moved), next(ids)
            )
        )
    start(to_chunk)

    arrive(gather1)
    gather2 = []
    for dx, dy in zip(x_steps, y_steps):
        own0, own1 = rows.at[0, y], rows.at[1, x]
        gather2.append(remote(own0, own0, at(**step("vir_2", y, dy, ny)), next(ids)))
        gather2.append(remote(own1, own1, at(**step("vir_0", x, dx, nx)), next(ids)))
    start(gather2)

    for copy in amp_loads:
        copy.wait()

    def split_amp(s, carry):
        base = pl.multiple_of(s * slab, slab)
        chunk = amp_raw[pl.ds(base, slab)].astype(F32)
        for n in range(pairs // LANES):
            amp_wide[n] = chunk[:, :, n * LANES : (n + 1) * LANES].reshape(slab * R, LANES)
        for d in range(R):
            for n in range(pairs // LANES):
                amp_d[d, pl.ds(base, slab), n * LANES : (n + 1) * LANES] = amp_wide[
                    n, pl.ds(d, slab, stride=R), :
                ].astype(BF16)
        return carry

    lax.fori_loop(0, nx, split_amp, 0)

    arrive(to_chunk)
    total = part[h * nk + k]
    for n in range(len(z_steps)):
        total = total + part_recv[n]
    mid = total.shape[0] // 2
    c1[0], c1[1] = total[:mid], total[mid:]
    sum1 = []
    for dx, dy in zip(x_steps, y_steps):
        sum1.append(
            remote(c1.at[0], c1_recv.at[0, dx - 1], at(**step("vir_0", x, dx, nx)), next(ids))
        )
        sum1.append(
            remote(c1.at[1], c1_recv.at[1, dy - 1], at(**step("vir_2", y, dy, ny)), next(ids))
        )
    start(sum1)

    arrive(gather2)
    for s in range(nx):
        low = rows[0, :, s].astype(F32).reshape(part_rows, pc)
        high = rows[1, s].astype(F32).reshape(part_rows, pc)
        row_lhs[:, s * slab : (s + 1) * slab] = jnp.concatenate([low, high], axis=0).T.astype(BF16)

    def make_half(d, carry):
        half[pl.ds(pl.multiple_of(d * pc, pc), pc), :] = jnp.dot(
            row_lhs[...], amp_d[d], preferred_element_type=F32
        ).astype(BF16)
        return carry

    lax.fori_loop(0, R, make_half, 0)

    swap = []
    for c in range(nl):
        full = jnp.dot(factor_t[c], half[...], preferred_element_type=F32)
        for n in range(nk):
            grid[c, n] = full[:, n * LANES : (n + 1) * LANES].reshape(nx, ny, R, LANES)
        swap.append(
            remote(grid.at[c, 1 - k], grid_recv.at[c], at(**step("vec", k, 1, nk)), next(ids))
        )
        start(swap[-1:])

    scatter1 = []
    for c in range(nl):
        arrive(swap[c : c + 1])
        wide[c] = grid[c, k] + grid_recv[c]
        if c == 0:
            stage[0] = wide[0].astype(BF16)
        else:
            for s in range(nx):
                for t in range(ny):
                    stage[1, t, s] = wide[1, s, t].astype(BF16)
        copies = []
        for d in x_steps if c == 0 else y_steps:
            moved = step("vir_0", x, d, nx) if c == 0 else step("vir_2", y, d, ny)
            there = moved["vir_0"] if c == 0 else moved["vir_2"]
            copies.append(
                remote(stage.at[c, there], stage_recv.at[c, d - 1], at(**moved), next(ids))
            )
        start(copies)
        scatter1.append(copies)

    arrive(sum1)
    for c in range(2):
        total = c1[c]
        for d in range(nx - 1):
            total = total + c1_recv[c, d]
        c2[c] = total
    sum2 = []
    for dx, dy in zip(x_steps, y_steps):
        sum2.append(
            remote(c2.at[0], c2_recv.at[0, dy - 1], at(**step("vir_2", y, dy, ny)), next(ids))
        )
        sum2.append(
            remote(c2.at[1], c2_recv.at[1, dx - 1], at(**step("vir_0", x, dx, nx)), next(ids))
        )
    start(sum2)

    scatter2 = []
    for c in range(nl):
        arrive(scatter1[c])
        total = wide[0, x] if c == 0 else wide[1, :, y]
        for d in range(nx - 1):
            total = total + stage_recv[c, d].astype(F32)
        second[c] = total
        copies = []
        for d in y_steps if c == 0 else x_steps:
            moved = step("vir_2", y, d, ny) if c == 0 else step("vir_0", x, d, nx)
            there = moved["vir_2"] if c == 0 else moved["vir_0"]
            copies.append(
                remote(second.at[c, there], second_recv.at[c, d - 1], at(**moved), next(ids))
            )
        start(copies)
        scatter2.append(copies)

    arrive(sum2)
    for c in range(2):
        total = c2[c]
        for d in range(nx - 1):
            total = total + c2_recv[c, d]
        c3[c * mid : (c + 1) * mid] = total
    sum3 = [remote(c3, c3_recv, at(**step("vir_1", l, 1, nl)), next(ids))]
    start(sum3)
    arrive(sum3)
    coupling = c3[...] + c3_recv[...]
    occ = coupling.shape[0]
    spread = jnp.broadcast_to(coupling[:, None, :], (occ, R, pc)).reshape(occ * R, pc)
    pairs_load.wait()
    second_count = ov_pairs.shape[0]
    ov = pairs_v[...].astype(F32).reshape(second_count * R, pc).astype(BF16)
    every = lax.dot_general(
        ov, spread.astype(BF16), (((1,), (1,)), ((), ())), preferred_element_type=F32
    )
    lane_j = lax.rem(lax.broadcasted_iota(jnp.int32, (R, pairs), 1), second_count)
    term = jnp.zeros((R, pairs), F32)
    for j in range(second_count):
        term = term + jnp.where(lane_j == j, every[j * R : (j + 1) * R], 0.0)
    for n in range(nk):
        cyc[n] = term[:, n * LANES : (n + 1) * LANES]
    swap_cyc = [remote(cyc.at[1 - k], cyc_recv, at(**step("vec", k, 1, nk)), next(ids))]
    start(swap_cyc)

    width = residual_ref.shape[1]
    per_half = LANES // width
    q = h * nk + k
    line = lax.broadcasted_iota(jnp.int32, (R, width), 0)
    lane = lax.broadcasted_iota(jnp.int32, (R, width), 1)
    slab_start = ((x * nl + l) * ny + y) * R
    virtual = jnp.zeros((R, width), F32)
    for r in range(R):
        virtual = jnp.where(line == r, eps_vir[slab_start + r], virtual)
    first_occ = jnp.zeros((R, width), F32)
    for n in range(width // second_count):
        first_occ = jnp.where(
            lane // second_count == n, eps_occ[q * (width // second_count) + n], first_occ
        )
    second_occ = jnp.zeros((R, width), F32)
    for n in range(second_count):
        second_occ = jnp.where(lax.rem(lane, second_count) == n, eps_occ[n], second_occ)
    denominator = (eps_vir[0] + virtual) - first_occ - second_occ

    arrive(swap_cyc)
    cycle_half = cyc[k] + cyc_recv[...]
    for c in range(nl):
        arrive(scatter2[c])
        total = second[0, y] if c == 0 else second[1, x]
        for d in range(nx - 1):
            total = total + second_recv[c, d]
        third[c] = total + jnp.where(l == c, cycle_half, 0.0)

    base_id = next(ids)
    mine = h * nl + l
    finals = []
    for m in range(per_half):
        for c in range(nl):
            there = k * per_half + m
            th, tk = there // nk, lax.rem(there, nk)
            away = jnp.logical_not((th == h) & (tk == k) & (c == l))
            copy = pltpu.make_async_remote_copy(
                src_ref=third.at[c],
                dst_ref=third_recv.at[mine],
                send_sem=send_sem.at[base_id + m * nl + c],
                recv_sem=recv_sem.at[base_id + mine],
                device_id=at(ph=th, vec=tk, vir_1=jnp.int32(c)),
                device_id_type=pl.DeviceIdType.MESH,
            )
            finals.append((away, copy))
            pl.when(away)(copy.start)
    own_source = q // per_half == k

    @pl.when(own_source)
    def _():
        third_recv[mine] = third[l]

    for s in range(nh * nl):
        from_other = jnp.logical_not(own_source & (mine == s))
        copy = pltpu.make_async_remote_copy(
            src_ref=third.at[0],
            dst_ref=third_recv.at[s],
            send_sem=send_sem.at[base_id],
            recv_sem=recv_sem.at[base_id + s],
            device_id=at(**step("vir_1", l, 1, nl)),
            device_id_type=pl.DeviceIdType.MESH,
        )
        pl.when(from_other)(copy.wait_recv)

    total = third_recv[0]
    for s in range(1, nh * nl):
        total = total + third_recv[s]
    mine_lanes = lax.rem(q, per_half)
    result = jnp.zeros((R, width), F32)
    for m in range(per_half):
        result = jnp.where(mine_lanes == m, total[:, m * width : (m + 1) * width], result)
    rounded = result.astype(BF16)
    residual_ref[...] = rounded
    update_ref[...] = rounded.astype(F32) / denominator

    for copy in sent:
        copy.wait_send()
    for away, copy in finals:
        pl.when(away)(copy.wait_send)


def local(
    sizes,
    vv_factor,
    ladder_amp,
    cycle_amp,
    ov_slots,
    owner_of,
    slot_of,
    ov_pairs,
    eps_vir,
    eps_occ,
):
    nx, nl, ny, nh, nk = sizes
    pc, _, virtuals = vv_factor.shape
    pairs = ladder_amp.shape[2]
    capacity, chol, part_w = ov_slots.shape
    occ = cycle_amp.shape[1]
    second_count = ov_pairs.shape[1]
    slots_t = jnp.transpose(ov_slots, (0, 2, 1)).reshape(capacity * part_w, chol)
    pairs_t = jnp.transpose(ov_pairs, (1, 2, 0))
    slab = nl * ny * R
    width = pairs // (nh * nk)
    steps = nx - 1
    VM = pltpu.VMEM
    scratch = [
        VM((nx, pc, R, slab), BF16),
        VM((pc * R, slab), F32),
        VM((nl, nx * ny * R, R * pc), BF16),
        VM(ladder_amp.shape, BF16),
        VM((pairs // LANES, slab * R, LANES), F32),
        VM((R, virtuals, pairs), BF16),
        VM((nl, nx, ny, R, pc), BF16),
        VM((pc, virtuals), BF16),
        VM((R * pc, pairs), BF16),
        VM(slots_t.shape, BF16),
        VM(cycle_amp.shape, BF16),
        VM(pairs_t.shape, BF16),
        VM((nh, 2, occ, 2 * part_w), BF16),
        VM((nh - 1, 2, occ, 2 * part_w), BF16),
        VM((nh * nk, occ, pc), F32),
        VM((nh * nk - 1, occ, pc), F32),
        VM((2, occ // 2, pc), F32),
        VM((2, steps, occ // 2, pc), F32),
        VM((2, occ // 2, pc), F32),
        VM((2, steps, occ // 2, pc), F32),
        VM((occ, pc), F32),
        VM((occ, pc), F32),
        VM((nk, R, LANES), F32),
        VM((R, LANES), F32),
        VM((nl, nk, nx, ny, R, LANES), F32),
        VM((nl, nx, ny, R, LANES), F32),
        VM((nl, nx, ny, R, LANES), F32),
        VM((nl, nx, ny, R, LANES), BF16),
        VM((nl, steps, ny, R, LANES), BF16),
        VM((nl, ny, R, LANES), F32),
        VM((nl, steps, R, LANES), F32),
        VM((nl, R, LANES), F32),
        VM((nh * nl, R, LANES), F32),
        pltpu.SemaphoreType.DMA((2 * nx + 3,)),
        pltpu.SemaphoreType.DMA((128,)),
        pltpu.SemaphoreType.DMA((128,)),
    ]
    hbm = pl.BlockSpec(memory_space=pltpu.MemorySpace.HBM)
    smem = pl.BlockSpec(memory_space=pltpu.SMEM)
    vmem = pl.BlockSpec(memory_space=pltpu.VMEM)
    return pl.pallas_call(
        functools.partial(body, sizes),
        out_shape=(
            jax.ShapeDtypeStruct((R, width), BF16),
            jax.ShapeDtypeStruct((R, width), F32),
        ),
        in_specs=[hbm, hbm, hbm, hbm, smem, smem, hbm, smem, smem],
        out_specs=(vmem, vmem),
        scratch_shapes=scratch,
        compiler_params=pltpu.CompilerParams(
            collective_id=0, has_side_effects=True, vmem_limit_bytes=63 * 1024 * 1024
        ),
    )(
        vv_factor,
        ladder_amp,
        cycle_amp,
        slots_t,
        owner_of,
        slot_of,
        pairs_t,
        eps_vir,
        eps_occ,
    )


def build(devices, sizes):
    torus = Mesh(devices.reshape(sizes), AXES)
    placed = (
        P(("ph", "vec"), VIR, None),
        P(None, VIR, None),
        P(VIR_PH, None, "vec"),
        P(VIR_PH, None, "vec"),
        P(VIR_PH),
        P(VIR_PH),
        P(("ph", "vec"), None, VIR),
        P(),
        P(),
    )
    return jax.shard_map(
        functools.partial(local, sizes),
        mesh=torus,
        in_specs=placed,
        out_specs=(P(VIR, ("ph", "vec")), P(VIR, ("ph", "vec"))),
        check_vma=False,
    )


def solution(mesh):
    return build(mesh.devices, (8, 2, 8, mesh.shape["ph"], mesh.shape["vec"]))
```

```python
import functools

import jax
import jax.numpy as jnp
from jax import lax
from jax.experimental import pallas as pl
from jax.experimental.pallas import tpu as pltpu
from jax.sharding import Mesh
from jax.sharding import PartitionSpec as P

AXES = ("vir_0", "vir_1", "vir_2", "ph", "vec")
VIR = ("vir_0", "vir_1", "vir_2")
VIR_PH = ("vir_0", "vir_1", "vir_2", "ph")
F32 = jnp.float32
BF16 = jnp.bfloat16
R = 8
LANES = 128


def far_first(count):
    return sorted(range(1, count), key=lambda d: -min(d, count - d))


def slot_at(delta, count):
    return jnp.where(delta * 2 <= count, jnp.maximum(2 * delta - 1, 0), 2 * (count - delta))


def slot_order(count):
    order = [0]
    for d in range(1, count // 2 + 1):
        order += [d, count - d] if 2 * d < count else [d]
    return order


def body(
    sizes,
    factor,
    amp,
    cycle_amp,
    ov_slots,
    owner_of,
    slot_of,
    ov_pairs,
    eps_vir,
    eps_occ,
    out_ref,
    out_v,
    owner_s,
    slot_s,
    eps_vir_s,
    eps_occ_s,
    factor_raw,
    factor_wide,
    factor_t,
    amp_raw,
    amp_wide,
    amp_d,
    rows,
    row_lhs,
    half_sum,
    half,
    slots_v,
    cyc_v,
    pairs_v,
    blk_send,
    blk_recv,
    part,
    part_recv,
    c1,
    c1_recv,
    c2,
    c2_recv,
    cyc,
    cyc_recv,
    grid,
    grid_recv,
    wide,
    stage,
    stage_recv,
    second,
    second_recv,
    third,
    third_recv,
    tally,
    load_sem,
    send_sem,
    recv_sem,
):
    nx, nl, ny, nh, nk = sizes
    pc = factor.shape[0]
    pairs = amp.shape[2]
    slab = nl * ny * R
    part_rows = ny * R
    x, l, y, h, k = (lax.axis_index(a) for a in AXES)
    me = {"vir_0": x, "vir_1": l, "vir_2": y, "ph": h, "vec": k}

    def at(**moved):
        return tuple(moved.get(a, me[a]) for a in AXES)

    def step(axis, value, d, count):
        return {axis: lax.rem(value + d, count)}

    ids = iter(range(1000))

    def remote(src, dst, target, slot):
        return pltpu.make_async_remote_copy(
            src_ref=src,
            dst_ref=dst,
            send_sem=send_sem.at[0],
            recv_sem=recv_sem.at[slot],
            device_id=target,
            device_id_type=pl.DeviceIdType.MESH,
        )

    unit = R * pc * 2
    sent_units = []

    def exchange(copies):
        slot = next(ids)
        units = 0
        for src, dst, moved in copies:
            remote(src, dst, at(**moved), slot).start()
            units += src.size * src.dtype.itemsize // unit
        sent_units.append(units)
        whole = tally.at[pl.ds(0, units)]
        return remote(whole, whole, at(**copies[0][2]), slot)

    x_steps, y_steps = far_first(nx), far_first(ny)

    z_steps = [
        (dl, dh, dk)
        for dh in sorted(range(nh), key=lambda d: -min(d, nh - d))
        for dl in range(nl)
        for dk in range(nk)
        if dl or dh or dk
    ]
    z_partners = [
        {**step("vir_1", l, dl, nl), **step("ph", h, dh, nh), **step("vec", k, dk, nk)}
        for dl, dh, dk in z_steps
    ]

    loads = []

    def load(whole, *copies):
        sem = load_sem.at[len(loads)]
        for src, dst in copies:
            pltpu.make_async_copy(src, dst, sem).start()
        loads.append(pltpu.make_async_copy(whole, whole, sem))
        return loads[-1]

    def slab_copy(s):
        return factor.at[:, :, pl.ds(s * slab, slab)], factor_raw.at[s]

    first_load = load(factor_raw.at[0], slab_copy(0))
    block_loads = [
        load(owner_s, (owner_of, owner_s)),
        load(slot_s, (slot_of, slot_s)),
        load(cyc_v, (cycle_amp, cyc_v)),
    ]

    barrier = pltpu.get_barrier_semaphore()
    partners = []
    for dx, dy in zip(x_steps, y_steps):
        for dl in reversed(range(nl)):
            partners.append({**step("vir_0", x, dx, nx), **step("vir_1", l, dl, nl)})
            partners.append({**step("vir_2", y, dy, ny), **step("vir_1", l, dl, nl)})
    for moved in partners + z_partners:
        pl.semaphore_signal(
            barrier, inc=1, device_id=at(**moved), device_id_type=pl.DeviceIdType.MESH
        )

    slots_load = load(slots_v, (ov_slots, slots_v))
    factor_load = load(factor_raw.at[1:], *[slab_copy(s) for s in range(1, nx)])
    amp_load = load(
        amp_raw,
        *[
            (amp.at[pl.ds(s * slab, slab)], amp_raw.at[pl.ds(s * slab, slab)])
            for s in range(nx)
        ],
    )
    late_loads = [
        load(pairs_v, (ov_pairs, pairs_v)),
        load(eps_vir_s, (eps_vir, eps_vir_s)),
        load(eps_occ_s, (eps_occ, eps_occ_s)),
    ]

    first_load.wait()
    first = factor_raw[0].astype(F32)[:, :, :1]
    lane_of = lax.broadcasted_iota(jnp.int32, (pc, R, pc), 2)
    row_of = lax.broadcasted_iota(jnp.int32, (pc, R, pc), 0)
    piece = jnp.sum(jnp.where(lane_of == row_of, first, 0.0), axis=0).astype(BF16)
    outer = jnp.where(l == 0, y, x)
    inner = jnp.where(l == 0, x, y)
    rows[l, outer, inner] = piece

    for copy in block_loads:
        copy.wait()
    blocks = [jnp.concatenate([cyc_v[n].astype(F32)] * 2, axis=1) for n in range(2)]
    lane_half = (
        lax.broadcasted_iota(jnp.int32, blocks[0].shape, 1) >= blocks[0].shape[1] // 2
    ).astype(jnp.int32)
    for target in range(nh):
        for pair in range(2):
            total = jnp.zeros_like(blocks[0])
            for n in range(2):
                wanted = jnp.where(owner_s[n] == target, slot_s[n], -1)
                total = total + jnp.where(lane_half + 2 * pair == wanted, blocks[n], 0.0)
            blk_send[target, pair] = total.astype(BF16)

    pl.semaphore_wait(barrier, len(partners) + len(z_partners))

    pick = rows.at[l, outer, inner]
    copies = []
    for d in far_first(nx) + [0]:
        for dl in reversed(range(nl)):
            if d or dl:
                moved = {
                    "vir_0": lax.rem(x + d * (1 - l), nx),
                    "vir_2": lax.rem(y + d * l, ny),
                    **step("vir_1", l, dl, nl),
                }
                copies.append((pick, pick, moved))
    gather1 = exchange(copies)
    owners = []
    for d in far_first(nh):
        moved = step("ph", h, d, nh)
        owners.append((blk_send.at[moved["ph"]], blk_recv.at[d - 1], moved))
    to_owner = exchange(owners)

    factor_load.wait()

    def turn_factor(s, carry):
        factor_wide[...] = factor_raw[s].astype(F32).reshape(factor_wide.shape)
        base = pl.multiple_of(s * part_rows, part_rows)
        for d in range(R):
            turned = factor_wide[pl.ds(d, pc, stride=R), :].T.astype(BF16)
            for c in range(nl):
                factor_t[c, pl.ds(base, part_rows), d * pc : (d + 1) * pc] = turned[
                    c * part_rows : (c + 1) * part_rows
                ]
        return carry

    lax.fori_loop(0, nx, turn_factor, 0)

    order_x, order_y = slot_order(nx), slot_order(ny)
    groups = [(0, nx // 2), (nx // 2, nx * 3 // 4), (nx * 3 // 4, nx)] if nx > 2 else [(0, 2)]

    gather1.wait_recv()
    gather2 = []
    for low_slot, high_slot in reversed(groups):
        copies = []
        for dx, dy in zip(x_steps, y_steps):
            own0, own1 = rows.at[0, y], rows.at[1, x]
            if low_slot <= order_y.index(ny - dy) < high_slot:
                copies.append((own0, own0, step("vir_2", y, dy, ny)))
                copies.append((own1, own1, step("vir_0", x, dx, nx)))
        gather2.insert(0, exchange(copies))

    slots_load.wait()
    to_owner.wait_recv()
    arranged = blk_send[h].astype(F32)
    for d in range(nh - 1):
        arranged = arranged + blk_recv[d].astype(F32)
    arranged = arranged.astype(BF16)
    depth = slots_v.shape[0] // 2
    for q in range(nh * nk):
        chunk = slice(q * pc, (q + 1) * pc)
        part[q] = (
            jnp.dot(arranged[0], slots_v[:depth, chunk], preferred_element_type=F32)
            + jnp.dot(arranged[1], slots_v[depth:, chunk], preferred_element_type=F32)
        ).astype(BF16)
    copies = []
    for n, moved in enumerate(z_partners):
        copies.append((part.at[moved["ph"] * nk + moved["vec"]], part_recv.at[n], moved))
    to_chunk = exchange(copies)

    amp_load.wait()

    def split_amp(s, carry):
        for u in range(2):
            chunk = amp_raw[pl.ds(pl.multiple_of((2 * s + u) * slab, slab), slab)].astype(F32)
            for n in range(pairs // LANES):
                amp_wide[u, n] = chunk[:, :, n * LANES : (n + 1) * LANES].reshape(slab * R, LANES)
        for d in range(R):
            for n in range(pairs // LANES):
                columns = slice(n * LANES, (n + 1) * LANES)
                for t in range(ny):
                    both = [amp_wide[u, n, pl.ds(t * R * R + d, R, stride=R), :] for u in range(2)]
                    place = slot_at(lax.rem(t - y + ny, ny), ny)
                    amp_d[d, place, pl.ds(pl.multiple_of(s * 2 * R, 2 * R), 2 * R), columns] = (
                        jnp.concatenate(both, axis=0).astype(BF16)
                    )
                for u in range(2):
                    place = slot_at(lax.rem(2 * s + u - x + nx, nx), nx)
                    amp_d[d, place, part_rows:, columns] = amp_wide[
                        u, n, pl.ds(part_rows * R + d, part_rows, stride=R), :
                    ].astype(BF16)
        return carry

    lax.fori_loop(0, nx // 2, split_amp, 0)

    mid = c1.shape[1]
    for index, (low_slot, high_slot) in enumerate(groups):
        gather2[index].wait_recv()
        for s in range(low_slot, high_slot):
            low = rows[0, lax.rem(y + order_y[s], ny)].astype(F32).reshape(part_rows, pc)
            high = rows[1, lax.rem(x + order_x[s], nx)].astype(F32).reshape(part_rows, pc)
            row_lhs[:, s * slab : (s + 1) * slab] = (
                jnp.concatenate([low, high], axis=0).T.astype(BF16)
            )

        def make_half(d, carry):
            lines = pl.ds(pl.multiple_of(d * pc, pc), pc)
            depth = (high_slot - low_slot) * slab
            value = jnp.dot(
                row_lhs[:, low_slot * slab : high_slot * slab],
                amp_d[d, low_slot:high_slot].reshape(depth, pairs),
                preferred_element_type=F32,
            )
            if index:
                value = half_sum[lines, :] + value
            if index == len(groups) - 1:
                half[lines, :] = value.astype(BF16)
            else:
                half_sum[lines, :] = value
            return carry

        lax.fori_loop(0, R, make_half, 0, unroll=True)

    swap = []
    for c in range(nl):
        full = jnp.dot(factor_t[c], half[...], preferred_element_type=F32)
        for n in range(nk):
            grid[c, n] = full[:, n * LANES : (n + 1) * LANES].reshape(nx, ny, R, LANES)
        swap.append(
            exchange([(grid.at[c, 1 - k], grid_recv.at[c], step("vec", k, 1, nk))])
        )
        if c == 0:
            to_chunk.wait_recv()
            total = part[h * nk + k].astype(F32)
            for n in range(len(z_partners)):
                total = total + part_recv[n].astype(F32)
            c1[0], c1[1] = total[:mid], total[mid:]
            copies = []
            for dx, dy in zip(x_steps, y_steps):
                copies.append((c1.at[0], c1_recv.at[0, dx - 1], step("vir_0", x, dx, nx)))
                copies.append((c1.at[1], c1_recv.at[1, dy - 1], step("vir_2", y, dy, ny)))
            sum1 = exchange(copies)

    scatter1 = []
    for c in range(nl):
        swap[c].wait_recv()
        wide[c] = grid[c, k] + grid_recv[c]
        if c == 0:
            stage[0] = wide[0].astype(BF16)
        else:
            for s in range(nx):
                for t in range(ny):
                    stage[1, t, s] = wide[1, s, t].astype(BF16)
        copies = []
        for d in x_steps if c == 0 else y_steps:
            moved = step("vir_0", x, d, nx) if c == 0 else step("vir_2", y, d, ny)
            there = moved["vir_0"] if c == 0 else moved["vir_2"]
            copies.append((stage.at[c, there], stage_recv.at[c, d - 1], moved))
        scatter1.append(exchange(copies))

    sum1.wait_recv()
    for c in range(2):
        total = c1[c]
        for d in range(nx - 1):
            total = total + c1_recv[c, d]
        c2[c] = total
    copies = []
    for dx, dy in zip(x_steps, y_steps):
        copies.append((c2.at[0], c2_recv.at[0, dy - 1], step("vir_2", y, dy, ny)))
        copies.append((c2.at[1], c2_recv.at[1, dx - 1], step("vir_0", x, dx, nx)))
    sum2 = exchange(copies)

    scatter2 = []
    for c in range(nl):
        scatter1[c].wait_recv()
        total = wide[0, x] if c == 0 else wide[1, :, y]
        for d in range(nx - 1):
            total = total + stage_recv[c, d].astype(F32)
        second[c] = total
        copies = []
        for d in y_steps if c == 0 else x_steps:
            moved = step("vir_2", y, d, ny) if c == 0 else step("vir_0", x, d, nx)
            there = moved["vir_2"] if c == 0 else moved["vir_0"]
            copies.append((second.at[c, there], second_recv.at[c, d - 1], moved))
        scatter2.append(exchange(copies))

    sum2.wait_recv()
    both = []
    for c in range(2):
        total = c2[c]
        for d in range(nx - 1):
            total = total + c2_recv[c, d]
        both.append(total)
    coupling = jnp.concatenate(both, axis=0)
    occ = coupling.shape[0]
    spread = jnp.broadcast_to(coupling[:, None, :], (occ, R, pc)).reshape(occ * R, pc)
    for copy in late_loads:
        copy.wait()
    second_count = ov_pairs.shape[0]
    ov = pairs_v[...].astype(F32).reshape(second_count * R, pc).astype(BF16)
    every = lax.dot_general(
        ov, spread.astype(BF16), (((1,), (1,)), ((), ())), preferred_element_type=F32
    )
    lane_j = lax.rem(lax.broadcasted_iota(jnp.int32, (R, pairs), 1), second_count)
    term = jnp.zeros((R, pairs), F32)
    for j in range(second_count):
        term = term + jnp.where(lane_j == j, every[j * R : (j + 1) * R], 0.0)
    for n in range(nk):
        cyc[n] = term[:, n * LANES : (n + 1) * LANES]
    swap_cyc = exchange([(cyc.at[1 - k], cyc_recv, step("vec", k, 1, nk))])

    width = out_ref.shape[2]
    per_half = LANES // width
    q = h * nk + k
    line = lax.broadcasted_iota(jnp.int32, (R, width), 0)
    lane = lax.broadcasted_iota(jnp.int32, (R, width), 1)
    slab_start = ((x * nl + l) * ny + y) * R
    virtual = jnp.zeros((R, width), F32)
    for r in range(R):
        virtual = jnp.where(line == r, eps_vir_s[slab_start + r], virtual)
    first_occ = jnp.zeros((R, width), F32)
    for n in range(width // second_count):
        first_occ = jnp.where(
            lane // second_count == n, eps_occ_s[q * (width // second_count) + n], first_occ
        )
    second_occ = jnp.zeros((R, width), F32)
    for n in range(second_count):
        second_occ = jnp.where(lax.rem(lane, second_count) == n, eps_occ_s[n], second_occ)
    denominator = (eps_vir_s[0] + virtual) - first_occ - second_occ

    swap_cyc.wait_recv()
    cycle_half = cyc[k] + cyc_recv[...]
    for c in range(nl):
        scatter2[c].wait_recv()
        total = second[0, y] if c == 0 else second[1, x]
        for d in range(nx - 1):
            total = total + second_recv[c, d]
        third[c] = total + jnp.where(l == c, cycle_half, 0.0)

    last = next(ids)
    mine = h * nl + l
    own_source = q // per_half == k
    for m in range(per_half):
        for c in range(nl):
            there = k * per_half + m
            th, tk = there // nk, lax.rem(there, nk)
            away = jnp.logical_not((th == h) & (tk == k) & (c == l))
            copy = pltpu.make_async_remote_copy(
                src_ref=third.at[c],
                dst_ref=third_recv.at[mine],
                send_sem=send_sem.at[1],
                recv_sem=recv_sem.at[last],
                device_id=at(ph=th, vec=tk, vir_1=jnp.int32(c)),
                device_id_type=pl.DeviceIdType.MESH,
            )
            pl.when(away)(copy.start)

    @pl.when(own_source)
    def _():
        third_recv[mine] = third[l]

    def finals(count):
        whole = third_recv.at[pl.ds(0, count)]
        return pltpu.make_async_remote_copy(
            src_ref=whole,
            dst_ref=whole,
            send_sem=send_sem.at[1],
            recv_sem=recv_sem.at[last],
            device_id=at(**step("vir_1", l, 1, nl)),
            device_id_type=pl.DeviceIdType.MESH,
        )

    others = per_half * nl

    whole = tally.at[pl.ds(0, sum(sent_units))]
    remote(whole, whole, at(**step("vec", k, 1, nk)), 0).wait_send()
    pl.when(own_source)(finals(others - 1).wait_recv)
    pl.when(jnp.logical_not(own_source))(finals(others).wait_recv)

    total = third_recv[0]
    for s in range(1, nh * nl):
        total = total + third_recv[s]
    mine_lanes = lax.rem(q, per_half)
    result = jnp.zeros((R, width), F32)
    for m in range(per_half):
        result = jnp.where(mine_lanes == m, total[:, m * width : (m + 1) * width], result)
    out_v[0] = result.astype(BF16).astype(F32)
    out_v[1] = denominator
    final_copy = pltpu.make_async_copy(out_v, out_ref, load_sem.at[0])
    final_copy.start()
    pl.when(own_source)(finals(others - 1).wait_send)
    pl.when(jnp.logical_not(own_source))(finals(others).wait_send)
    final_copy.wait()


def local(
    sizes,
    vv_factor,
    ladder_amp,
    cycle_amp,
    ov_slots,
    owner_of,
    slot_of,
    ov_pairs,
    eps_vir,
    eps_occ,
):
    nx, nl, ny, nh, nk = sizes
    pc, _, virtuals = vv_factor.shape
    pairs = ladder_amp.shape[2]
    capacity, chol, part_w = ov_slots.shape
    occ = cycle_amp.shape[1]
    second_count = ov_pairs.shape[1]
    slots_t = jnp.transpose(ov_slots, (0, 2, 1)).reshape(capacity * part_w, chol)
    pairs_t = jnp.transpose(ov_pairs, (1, 2, 0))
    slab = nl * ny * R
    width = pairs // (nh * nk)
    steps = nx - 1
    VM = pltpu.VMEM
    scratch = [
        VM((2, R, width), F32),
        pltpu.SMEM(owner_of.shape, jnp.int32),
        pltpu.SMEM(slot_of.shape, jnp.int32),
        pltpu.SMEM(eps_vir.shape, F32),
        pltpu.SMEM(eps_occ.shape, F32),
        VM((nx, pc, R, slab), BF16),
        VM((pc * R, slab), F32),
        VM((nl, nx * ny * R, R * pc), BF16),
        VM(ladder_amp.shape, BF16),
        VM((2, pairs // LANES, slab * R, LANES), F32),
        VM((R, nx, slab, pairs), BF16),
        VM((nl, nx, ny, R, pc), BF16),
        VM((pc, virtuals), BF16),
        VM((R * pc, pairs), F32),
        VM((R * pc, pairs), BF16),
        VM(slots_t.shape, BF16),
        VM(cycle_amp.shape, BF16),
        VM(pairs_t.shape, BF16),
        VM((nh, 2, occ, 2 * part_w), BF16),
        VM((nh - 1, 2, occ, 2 * part_w), BF16),
        VM((nh * nk, occ, pc), BF16),
        VM((nh * nk * nl - 1, occ, pc), BF16),
        VM((2, occ // 2, pc), F32),
        VM((2, steps, occ // 2, pc), F32),
        VM((2, occ // 2, pc), F32),
        VM((2, steps, occ // 2, pc), F32),
        VM((nk, R, LANES), F32),
        VM((R, LANES), F32),
        VM((nl, nk, nx, ny, R, LANES), F32),
        VM((nl, nx, ny, R, LANES), F32),
        VM((nl, nx, ny, R, LANES), F32),
        VM((nl, nx, ny, R, LANES), BF16),
        VM((nl, steps, ny, R, LANES), BF16),
        VM((nl, ny, R, LANES), F32),
        VM((nl, steps, R, LANES), F32),
        VM((nl, R, LANES), F32),
        VM((nh * nl, R, LANES), F32),
        VM((1024, R, pc), BF16),
        pltpu.SemaphoreType.DMA((10,)),
        pltpu.SemaphoreType.DMA((2,)),
        pltpu.SemaphoreType.DMA((16,)),
    ]
    hbm = pl.BlockSpec(memory_space=pltpu.MemorySpace.HBM)
    out = pl.pallas_call(
        functools.partial(body, sizes),
        out_shape=jax.ShapeDtypeStruct((2, R, width), F32),
        in_specs=[hbm] * 9,
        out_specs=hbm,
        scratch_shapes=scratch,
        compiler_params=pltpu.CompilerParams(
            collective_id=0, has_side_effects=True, vmem_limit_bytes=63 * 1024 * 1024
        ),
    )(
        vv_factor,
        ladder_amp,
        cycle_amp,
        slots_t,
        owner_of,
        slot_of,
        pairs_t,
        eps_vir,
        eps_occ,
    )
    residual = out[0].astype(BF16)
    return residual, residual.astype(F32) / out[1]


def build(devices, sizes):
    torus = Mesh(devices.reshape(sizes), AXES)
    placed = (
        P(("ph", "vec"), VIR, None),
        P(None, VIR, None),
        P(VIR_PH, None, "vec"),
        P(VIR_PH, None, "vec"),
        P(VIR_PH),
        P(VIR_PH),
        P(("ph", "vec"), None, VIR),
        P(),
        P(),
    )
    return jax.shard_map(
        functools.partial(local, sizes),
        mesh=torus,
        in_specs=placed,
        out_specs=(P(VIR, ("ph", "vec")), P(VIR, ("ph", "vec"))),
        check_vma=False,
    )


def solution(mesh):
    return build(mesh.devices, (8, 2, 8, mesh.shape["ph"], mesh.shape["vec"]))
```

```python
import functools

import jax
import jax.numpy as jnp
from jax import lax
from jax.experimental import pallas as pl
from jax.experimental.pallas import tpu as pltpu
from jax.sharding import Mesh
from jax.sharding import PartitionSpec as P

AXES = ("vir_0", "vir_1", "vir_2", "ph", "vec")
VIR = ("vir_0", "vir_1", "vir_2")
VIR_PH = ("vir_0", "vir_1", "vir_2", "ph")
F32 = jnp.float32
BF16 = jnp.bfloat16
R = 8
LANES = 128


def far_first(count):
    return sorted(range(1, count), key=lambda d: -min(d, count - d))


def slot_at(delta, count):
    return jnp.where(delta * 2 <= count, jnp.maximum(2 * delta - 1, 0), 2 * (count - delta))


def slot_order(count):
    order = [0]
    for d in range(1, count // 2 + 1):
        order += [d, count - d] if 2 * d < count else [d]
    return order


def body(
    sizes,
    factor,
    amp,
    cycle_amp,
    ov_slots,
    owner_of,
    slot_of,
    ov_pairs,
    eps_vir,
    eps_occ,
    out_ref,
    owner_s,
    slot_s,
    eps_vir_s,
    eps_occ_s,
    factor_raw,
    factor_wide,
    factor_t,
    amp_raw,
    amp_wide,
    amp_d,
    rows,
    row_lhs,
    half_sum,
    half,
    slots_v,
    cyc_v,
    pairs_v,
    blk_send,
    blk_recv,
    part,
    part_recv,
    c1,
    c1_recv,
    c2,
    c2_recv,
    cyc,
    cyc_recv,
    grid,
    grid_recv,
    wide,
    stage,
    stage_recv,
    second,
    second_recv,
    third,
    third_recv,
    tally,
    load_sem,
    send_sem,
    recv_sem,
):
    nx, nl, ny, nh, nk = sizes
    pc = factor.shape[0]
    pairs = amp.shape[2]
    slab = nl * ny * R
    part_rows = ny * R
    x, l, y, h, k = (lax.axis_index(a) for a in AXES)
    me = {"vir_0": x, "vir_1": l, "vir_2": y, "ph": h, "vec": k}

    def at(**moved):
        return tuple(moved.get(a, me[a]) for a in AXES)

    def step(axis, value, d, count):
        return {axis: lax.rem(value + d, count)}

    ids = iter(range(1000))

    def remote(src, dst, target, slot):
        return pltpu.make_async_remote_copy(
            src_ref=src,
            dst_ref=dst,
            send_sem=send_sem.at[0],
            recv_sem=recv_sem.at[slot],
            device_id=target,
            device_id_type=pl.DeviceIdType.MESH,
        )

    unit = R * pc * 2
    sent_units = []

    def exchange(copies):
        slot = next(ids)
        units = 0
        for src, dst, moved in copies:
            remote(src, dst, at(**moved), slot).start()
            units += src.size * src.dtype.itemsize // unit
        sent_units.append(units)
        whole = tally.at[pl.ds(0, units)]
        return remote(whole, whole, at(**copies[0][2]), slot)

    x_steps, y_steps = far_first(nx), far_first(ny)

    z_steps = [
        (dl, dh, dk)
        for dh in sorted(range(nh), key=lambda d: -min(d, nh - d))
        for dl in range(nl)
        for dk in range(nk)
        if dl or dh or dk
    ]
    z_partners = [
        {**step("vir_1", l, dl, nl), **step("ph", h, dh, nh), **step("vec", k, dk, nk)}
        for dl, dh, dk in z_steps
    ]
    z_hops = [nl * min(dh, nh - dh) + dl for dl, dh, dk in z_steps]

    loads = []

    def load(whole, *copies):
        sem = load_sem.at[len(loads)]
        for src, dst in copies:
            pltpu.make_async_copy(src, dst, sem).start()
        loads.append(pltpu.make_async_copy(whole, whole, sem))
        return loads[-1]

    def slab_copy(s):
        return factor.at[:, :, pl.ds(s * slab, slab)], factor_raw.at[s]

    first_load = load(factor_raw.at[0], slab_copy(0))
    block_loads = [
        load(owner_s, (owner_of, owner_s)),
        load(slot_s, (slot_of, slot_s)),
        load(cyc_v, (cycle_amp, cyc_v)),
    ]

    barrier = pltpu.get_barrier_semaphore()
    partners = list(zip(z_hops, z_partners))
    for dx, dy in zip(x_steps, y_steps):
        for dl in reversed(range(nl)):
            far_x, far_y = min(dx, nx - dx) + dl, min(dy, ny - dy) + dl
            partners.append((far_x, {**step("vir_0", x, dx, nx), **step("vir_1", l, dl, nl)}))
            partners.append((far_y, {**step("vir_2", y, dy, ny), **step("vir_1", l, dl, nl)}))
    for _, moved in sorted(partners, key=lambda partner: -partner[0]):
        pl.semaphore_signal(
            barrier, inc=1, device_id=at(**moved), device_id_type=pl.DeviceIdType.MESH
        )

    slots_load = load(slots_v, (ov_slots, slots_v))
    factor_load = load(factor_raw.at[1:], *[slab_copy(s) for s in range(1, nx)])
    amp_load = load(
        amp_raw,
        *[
            (amp.at[pl.ds(s * slab, slab)], amp_raw.at[pl.ds(s * slab, slab)])
            for s in range(nx)
        ],
    )
    late_loads = [
        load(pairs_v, (ov_pairs, pairs_v)),
        load(eps_vir_s, (eps_vir, eps_vir_s)),
        load(eps_occ_s, (eps_occ, eps_occ_s)),
    ]

    first_load.wait()
    first = factor_raw[0].astype(F32)[:, :, :1]
    lane_of = lax.broadcasted_iota(jnp.int32, (pc, R, pc), 2)
    row_of = lax.broadcasted_iota(jnp.int32, (pc, R, pc), 0)
    piece = jnp.sum(jnp.where(lane_of == row_of, first, 0.0), axis=0).astype(BF16)
    outer = jnp.where(l == 0, y, x)
    inner = jnp.where(l == 0, x, y)
    rows[l, outer, inner] = piece

    for copy in block_loads:
        copy.wait()
    blocks = [jnp.concatenate([cyc_v[n].astype(F32)] * 2, axis=1) for n in range(2)]
    lane_half = (
        lax.broadcasted_iota(jnp.int32, blocks[0].shape, 1) >= blocks[0].shape[1] // 2
    ).astype(jnp.int32)
    for target in range(nh):
        for pair in range(2):
            total = jnp.zeros_like(blocks[0])
            for n in range(2):
                wanted = jnp.where(owner_s[n] == target, slot_s[n], -1)
                total = total + jnp.where(lane_half + 2 * pair == wanted, blocks[n], 0.0)
            blk_send[target, pair] = total.astype(BF16)

    pl.semaphore_wait(barrier, len(partners))

    pick = rows.at[l, outer, inner]
    copies = []
    for d in far_first(nx) + [0]:
        for dl in reversed(range(nl)):
            if d or dl:
                moved = {
                    "vir_0": lax.rem(x + d * (1 - l), nx),
                    "vir_2": lax.rem(y + d * l, ny),
                    **step("vir_1", l, dl, nl),
                }
                copies.append((pick, pick, moved))
    gather1 = exchange(copies)
    owners = []
    for d in far_first(nh):
        moved = step("ph", h, d, nh)
        owners.append((blk_send.at[moved["ph"]], blk_recv.at[d - 1], moved))
    to_owner = exchange(owners)

    amp_load.wait()

    def split_amp(s, carry):
        for u in range(2):
            chunk = amp_raw[pl.ds(pl.multiple_of((2 * s + u) * slab, slab), slab)].astype(F32)
            for n in range(pairs // LANES):
                amp_wide[u, n] = chunk[:, :, n * LANES : (n + 1) * LANES].reshape(slab * R, LANES)
        for d in range(R):
            for n in range(pairs // LANES):
                columns = slice(n * LANES, (n + 1) * LANES)
                for t in range(ny):
                    both = [amp_wide[u, n, pl.ds(t * R * R + d, R, stride=R), :] for u in range(2)]
                    place = slot_at(lax.rem(t - y + ny, ny), ny)
                    amp_d[d, place, pl.ds(pl.multiple_of(s * 2 * R, 2 * R), 2 * R), columns] = (
                        jnp.concatenate(both, axis=0).astype(BF16)
                    )
                for u in range(2):
                    place = slot_at(lax.rem(2 * s + u - x + nx, nx), nx)
                    amp_d[d, place, part_rows:, columns] = amp_wide[
                        u, n, pl.ds(part_rows * R + d, part_rows, stride=R), :
                    ].astype(BF16)
        return carry

    lax.fori_loop(0, nx // 2, split_amp, 0)

    order_x, order_y = slot_order(nx), slot_order(ny)
    groups = [(0, nx // 2), (nx // 2, nx * 3 // 4), (nx * 3 // 4, nx)] if nx > 2 else [(0, 2)]

    gather1.wait_recv()
    gather2 = []
    for low_slot, high_slot in reversed(groups):
        copies = []
        for dx, dy in zip(x_steps, y_steps):
            own0, own1 = rows.at[0, y], rows.at[1, x]
            if low_slot <= order_y.index(ny - dy) < high_slot:
                copies.append((own0, own0, step("vir_2", y, dy, ny)))
                copies.append((own1, own1, step("vir_0", x, dx, nx)))
        gather2.insert(0, exchange(copies))

    slots_load.wait()
    to_owner.wait_recv()
    arranged = blk_send[h].astype(F32)
    for d in range(nh - 1):
        arranged = arranged + blk_recv[d].astype(F32)
    arranged = arranged.astype(BF16)
    depth = slots_v.shape[0] // 2
    for q in range(nh * nk):
        chunk = slice(q * pc, (q + 1) * pc)
        part[q] = (
            jnp.dot(arranged[0], slots_v[:depth, chunk], preferred_element_type=F32)
            + jnp.dot(arranged[1], slots_v[depth:, chunk], preferred_element_type=F32)
        ).astype(BF16)
    copies = []
    for n, moved in enumerate(z_partners):
        copies.append((part.at[moved["ph"] * nk + moved["vec"]], part_recv.at[n], moved))
    to_chunk = exchange(copies)

    factor_load.wait()

    def turn_factor(s, carry):
        factor_wide[...] = factor_raw[s].astype(F32).reshape(factor_wide.shape)
        base = pl.multiple_of(s * part_rows, part_rows)
        for d in range(R):
            turned = factor_wide[pl.ds(d, pc, stride=R), :].T.astype(BF16)
            for c in range(nl):
                factor_t[c, pl.ds(base, part_rows), d * pc : (d + 1) * pc] = turned[
                    c * part_rows : (c + 1) * part_rows
                ]
        return carry

    lax.fori_loop(0, nx, turn_factor, 0)

    mid = c1.shape[1]
    for index, (low_slot, high_slot) in enumerate(groups):
        gather2[index].wait_recv()
        for s in range(low_slot, high_slot):
            low = rows[0, lax.rem(y + order_y[s], ny)].astype(F32).reshape(part_rows, pc)
            high = rows[1, lax.rem(x + order_x[s], nx)].astype(F32).reshape(part_rows, pc)
            row_lhs[:, s * slab : (s + 1) * slab] = (
                jnp.concatenate([low, high], axis=0).T.astype(BF16)
            )

        def make_half(d, carry):
            lines = pl.ds(pl.multiple_of(d * pc, pc), pc)
            depth = (high_slot - low_slot) * slab
            value = jnp.dot(
                row_lhs[:, low_slot * slab : high_slot * slab],
                amp_d[d, low_slot:high_slot].reshape(depth, pairs),
                preferred_element_type=F32,
            )
            if index:
                value = half_sum[lines, :] + value
            if index == len(groups) - 1:
                half[lines, :] = value.astype(BF16)
            else:
                half_sum[lines, :] = value
            return carry

        lax.fori_loop(0, R, make_half, 0, unroll=True)

    swap = []
    for c in range(nl):
        full = jnp.dot(factor_t[c], half[...], preferred_element_type=F32)
        for n in range(nk):
            grid[c, n] = full[:, n * LANES : (n + 1) * LANES].reshape(nx, ny, R, LANES)
        swap.append(
            exchange([(grid.at[c, 1 - k], grid_recv.at[c], step("vec", k, 1, nk))])
        )

    to_chunk.wait_recv()
    total = part[h * nk + k].astype(F32)
    for n in range(len(z_partners)):
        total = total + part_recv[n].astype(F32)
    parts = [total[:mid], total[mid:]]
    c1[0], c1[1] = [p.astype(BF16) for p in parts]
    copies = []
    for dx, dy in zip(x_steps, y_steps):
        copies.append((c1.at[0], c1_recv.at[0, dx - 1], step("vir_0", x, dx, nx)))
        copies.append((c1.at[1], c1_recv.at[1, dy - 1], step("vir_2", y, dy, ny)))
    sum1 = exchange(copies)

    scatter1 = []
    for c in range(nl):
        swap[c].wait_recv()
        wide[c] = grid[c, k] + grid_recv[c]
        if c == 0:
            stage[0] = wide[0].astype(BF16)
        else:
            for s in range(nx):
                for t in range(ny):
                    stage[1, t, s] = wide[1, s, t].astype(BF16)
        copies = []
        for d in x_steps if c == 0 else y_steps:
            moved = step("vir_0", x, d, nx) if c == 0 else step("vir_2", y, d, ny)
            there = moved["vir_0"] if c == 0 else moved["vir_2"]
            copies.append((stage.at[c, there], stage_recv.at[c, d - 1], moved))
        scatter1.append(exchange(copies))

    sum1.wait_recv()
    for c in range(2):
        for d in range(nx - 1):
            parts[c] = parts[c] + c1_recv[c, d].astype(F32)
        c2[c] = parts[c].astype(BF16)
    copies = []
    for dx, dy in zip(x_steps, y_steps):
        copies.append((c2.at[0], c2_recv.at[0, dy - 1], step("vir_2", y, dy, ny)))
        copies.append((c2.at[1], c2_recv.at[1, dx - 1], step("vir_0", x, dx, nx)))
    sum2 = exchange(copies)

    scatter2 = []
    for c in range(nl):
        scatter1[c].wait_recv()
        total = wide[0, x] if c == 0 else wide[1, :, y]
        for d in range(nx - 1):
            total = total + stage_recv[c, d].astype(F32)
        second[c] = total
        copies = []
        for d in y_steps if c == 0 else x_steps:
            moved = step("vir_2", y, d, ny) if c == 0 else step("vir_0", x, d, nx)
            there = moved["vir_2"] if c == 0 else moved["vir_0"]
            copies.append((second.at[c, there], second_recv.at[c, d - 1], moved))
        scatter2.append(exchange(copies))

    sum2.wait_recv()
    both = []
    for c in range(2):
        total = parts[c]
        for d in range(nx - 1):
            total = total + c2_recv[c, d].astype(F32)
        both.append(total)
    coupling = jnp.concatenate(both, axis=0)
    occ = coupling.shape[0]
    spread = jnp.broadcast_to(coupling[:, None, :], (occ, R, pc)).reshape(occ * R, pc)
    for copy in late_loads:
        copy.wait()
    second_count = ov_pairs.shape[0]
    ov = pairs_v[...].astype(F32).reshape(second_count * R, pc).astype(BF16)
    every = lax.dot_general(
        ov, spread.astype(BF16), (((1,), (1,)), ((), ())), preferred_element_type=F32
    )
    lane_j = lax.rem(lax.broadcasted_iota(jnp.int32, (R, pairs), 1), second_count)
    term = jnp.zeros((R, pairs), F32)
    for j in range(second_count):
        term = term + jnp.where(lane_j == j, every[j * R : (j + 1) * R], 0.0)
    for n in range(nk):
        cyc[n] = term[:, n * LANES : (n + 1) * LANES]
    per_half = LANES // out_ref.shape[2]
    copies = []
    for (dl, dh, dk), moved in zip(z_steps, z_partners):
        if dl == 0:
            there = moved["ph"] * nk + moved["vec"]
            copies.append((cyc.at[there // per_half], cyc_recv.at[len(copies)], moved))
    to_pairs = exchange(copies)

    width = out_ref.shape[2]
    q = h * nk + k
    line = lax.broadcasted_iota(jnp.int32, (R, width), 0)
    lane = lax.broadcasted_iota(jnp.int32, (R, width), 1)
    slab_start = ((x * nl + l) * ny + y) * R
    virtual = jnp.zeros((R, width), F32)
    for r in range(R):
        virtual = jnp.where(line == r, eps_vir_s[slab_start + r], virtual)
    first_occ = jnp.zeros((R, width), F32)
    for n in range(width // second_count):
        first_occ = jnp.where(
            lane // second_count == n, eps_occ_s[q * (width // second_count) + n], first_occ
        )
    second_occ = jnp.zeros((R, width), F32)
    for n in range(second_count):
        second_occ = jnp.where(lax.rem(lane, second_count) == n, eps_occ_s[n], second_occ)
    denominator = (eps_vir_s[0] + virtual) - first_occ - second_occ

    for c in range(nl):
        scatter2[c].wait_recv()
        total = second[0, y] if c == 0 else second[1, x]
        for d in range(nx - 1):
            total = total + second_recv[c, d]
        third[c] = total

    last = next(ids)
    mine = h * nl + l
    own_source = q // per_half == k
    for m in range(per_half):
        for c in range(nl):
            there = k * per_half + m
            th, tk = there // nk, lax.rem(there, nk)
            away = jnp.logical_not((th == h) & (tk == k) & (c == l))
            copy = pltpu.make_async_remote_copy(
                src_ref=third.at[c],
                dst_ref=third_recv.at[mine],
                send_sem=send_sem.at[1],
                recv_sem=recv_sem.at[last],
                device_id=at(ph=th, vec=tk, vir_1=jnp.int32(c)),
                device_id_type=pl.DeviceIdType.MESH,
            )
            pl.when(away)(copy.start)

    @pl.when(own_source)
    def _():
        third_recv[mine] = third[l]

    def finals(count):
        whole = third_recv.at[pl.ds(0, count)]
        return pltpu.make_async_remote_copy(
            src_ref=whole,
            dst_ref=whole,
            send_sem=send_sem.at[1],
            recv_sem=recv_sem.at[last],
            device_id=at(**step("vir_1", l, 1, nl)),
            device_id_type=pl.DeviceIdType.MESH,
        )

    others = per_half * nl

    to_pairs.wait_recv()
    cycle_sum = cyc[q // per_half]
    for n in range(nh * nk - 1):
        cycle_sum = cycle_sum + cyc_recv[n]
    whole = tally.at[pl.ds(0, sum(sent_units))]
    remote(whole, whole, at(**step("vec", k, 1, nk)), 0).wait_send()
    pl.when(own_source)(finals(others - 1).wait_recv)
    pl.when(jnp.logical_not(own_source))(finals(others).wait_recv)

    total = cycle_sum
    for s in range(nh * nl):
        total = total + third_recv[s]
    mine_lanes = lax.rem(q, per_half)
    result = jnp.zeros((R, width), F32)
    for m in range(per_half):
        result = jnp.where(mine_lanes == m, total[:, m * width : (m + 1) * width], result)
    out_ref[0] = result.astype(BF16).astype(F32)
    out_ref[1] = denominator
    pl.when(own_source)(finals(others - 1).wait_send)
    pl.when(jnp.logical_not(own_source))(finals(others).wait_send)


def local(
    sizes,
    vv_factor,
    ladder_amp,
    cycle_amp,
    ov_slots,
    owner_of,
    slot_of,
    ov_pairs,
    eps_vir,
    eps_occ,
):
    nx, nl, ny, nh, nk = sizes
    pc, _, virtuals = vv_factor.shape
    pairs = ladder_amp.shape[2]
    capacity, chol, part_w = ov_slots.shape
    occ = cycle_amp.shape[1]
    second_count = ov_pairs.shape[1]
    slots_t = jnp.transpose(ov_slots, (0, 2, 1)).reshape(capacity * part_w, chol)
    pairs_t = jnp.transpose(ov_pairs, (1, 2, 0))
    slab = nl * ny * R
    width = pairs // (nh * nk)
    steps = nx - 1
    VM = pltpu.VMEM
    scratch = [
        pltpu.SMEM(owner_of.shape, jnp.int32),
        pltpu.SMEM(slot_of.shape, jnp.int32),
        pltpu.SMEM(eps_vir.shape, F32),
        pltpu.SMEM(eps_occ.shape, F32),
        VM((nx, pc, R, slab), BF16),
        VM((pc * R, slab), F32),
        VM((nl, nx * ny * R, R * pc), BF16),
        VM(ladder_amp.shape, BF16),
        VM((2, pairs // LANES, slab * R, LANES), F32),
        VM((R, nx, slab, pairs), BF16),
        VM((nl, nx, ny, R, pc), BF16),
        VM((pc, virtuals), BF16),
        VM((R * pc, pairs), F32),
        VM((R * pc, pairs), BF16),
        VM(slots_t.shape, BF16),
        VM(cycle_amp.shape, BF16),
        VM(pairs_t.shape, BF16),
        VM((nh, 2, occ, 2 * part_w), BF16),
        VM((nh - 1, 2, occ, 2 * part_w), BF16),
        VM((nh * nk, occ, pc), BF16),
        VM((nh * nk * nl - 1, occ, pc), BF16),
        VM((2, occ // 2, pc), BF16),
        VM((2, steps, occ // 2, pc), BF16),
        VM((2, occ // 2, pc), BF16),
        VM((2, steps, occ // 2, pc), BF16),
        VM((nk, R, LANES), F32),
        VM((nh * nk - 1, R, LANES), F32),
        VM((nl, nk, nx, ny, R, LANES), F32),
        VM((nl, nx, ny, R, LANES), F32),
        VM((nl, nx, ny, R, LANES), F32),
        VM((nl, nx, ny, R, LANES), BF16),
        VM((nl, steps, ny, R, LANES), BF16),
        VM((nl, ny, R, LANES), F32),
        VM((nl, steps, R, LANES), F32),
        VM((nl, R, LANES), F32),
        VM((nh * nl, R, LANES), F32),
        VM((1024, R, pc), BF16),
        pltpu.SemaphoreType.DMA((10,)),
        pltpu.SemaphoreType.DMA((2,)),
        pltpu.SemaphoreType.DMA((16,)),
    ]
    hbm = pl.BlockSpec(memory_space=pltpu.MemorySpace.HBM)
    out = pl.pallas_call(
        functools.partial(body, sizes),
        out_shape=pltpu.VMEM((2, R, width), F32),
        in_specs=[hbm] * 9,
        out_specs=pl.BlockSpec(memory_space=pltpu.VMEM),
        scratch_shapes=scratch,
        compiler_params=pltpu.CompilerParams(
            collective_id=0, has_side_effects=True, vmem_limit_bytes=63 * 1024 * 1024
        ),
    )(
        vv_factor,
        ladder_amp,
        cycle_amp,
        slots_t,
        owner_of,
        slot_of,
        pairs_t,
        eps_vir,
        eps_occ,
    )
    residual = out[0].astype(BF16)
    return residual, residual.astype(F32) / out[1]


def build(devices, sizes):
    torus = Mesh(devices.reshape(sizes), AXES)
    placed = (
        P(("ph", "vec"), VIR, None),
        P(None, VIR, None),
        P(VIR_PH, None, "vec"),
        P(VIR_PH, None, "vec"),
        P(VIR_PH),
        P(VIR_PH),
        P(("ph", "vec"), None, VIR),
        P(),
        P(),
    )
    return jax.shard_map(
        functools.partial(local, sizes),
        mesh=torus,
        in_specs=placed,
        out_specs=(P(VIR, ("ph", "vec")), P(VIR, ("ph", "vec"))),
        check_vma=False,
    )


def solution(mesh):
    return build(mesh.devices, (8, 2, 8, mesh.shape["ph"], mesh.shape["vec"]))
```

```python
import functools

import jax
import jax.numpy as jnp
from jax import lax
from jax.experimental import pallas as pl
from jax.experimental.pallas import tpu as pltpu
from jax.sharding import Mesh
from jax.sharding import PartitionSpec as P

AXES = ("vir_0", "vir_1", "vir_2", "ph", "vec")
VIR = ("vir_0", "vir_1", "vir_2")
VIR_PH = ("vir_0", "vir_1", "vir_2", "ph")
F32 = jnp.float32
BF16 = jnp.bfloat16
R = 8
LANES = 128


def far_first(count):
    return sorted(range(1, count), key=lambda d: -min(d, count - d))


def slot_at(delta, count):
    return jnp.where(delta * 2 <= count, jnp.maximum(2 * delta - 1, 0), 2 * (count - delta))


def slot_order(count):
    order = [0]
    for d in range(1, count // 2 + 1):
        order += [d, count - d] if 2 * d < count else [d]
    return order


def body(
    sizes,
    factor,
    amp,
    cycle_amp,
    ov_slots,
    owner_of,
    slot_of,
    ov_pairs,
    eps_vir,
    eps_occ,
    out_ref,
    owner_s,
    slot_s,
    eps_vir_s,
    eps_occ_s,
    factor_raw,
    factor_wide,
    factor_t,
    amp_raw,
    amp_wide,
    amp_d,
    rows,
    row_lhs,
    half_sum,
    half,
    slots_v,
    cyc_v,
    pairs_v,
    blk_send,
    blk_recv,
    part,
    part_recv,
    c1,
    c1_recv,
    c2,
    c2_recv,
    cyc,
    cyc_recv,
    grid,
    grid_send,
    grid_recv,
    wide,
    stage,
    stage_recv,
    second,
    second_recv,
    third,
    third_recv,
    tally,
    load_sem,
    send_sem,
    recv_sem,
):
    nx, nl, ny, nh, nk = sizes
    pc = factor.shape[0]
    pairs = amp.shape[2]
    slab = nl * ny * R
    part_rows = ny * R
    x, l, y, h, k = (lax.axis_index(a) for a in AXES)
    me = {"vir_0": x, "vir_1": l, "vir_2": y, "ph": h, "vec": k}

    def at(**moved):
        return tuple(moved.get(a, me[a]) for a in AXES)

    def step(axis, value, d, count):
        return {axis: lax.rem(value + d, count)}

    ids = iter(range(1000))

    def remote(src, dst, target, slot):
        return pltpu.make_async_remote_copy(
            src_ref=src,
            dst_ref=dst,
            send_sem=send_sem.at[0],
            recv_sem=recv_sem.at[slot],
            device_id=target,
            device_id_type=pl.DeviceIdType.MESH,
        )

    unit = R * pc * 2
    sent_units = []

    def exchange(copies):
        slot = next(ids)
        units = 0
        for src, dst, moved in copies:
            remote(src, dst, at(**moved), slot).start()
            units += src.size * src.dtype.itemsize // unit
        sent_units.append(units)
        whole = tally.at[pl.ds(0, units)]
        return remote(whole, whole, at(**copies[0][2]), slot)

    x_steps, y_steps = far_first(nx), far_first(ny)

    z_steps = [
        (dl, dh, dk)
        for dh in sorted(range(nh), key=lambda d: -min(d, nh - d))
        for dl in range(nl)
        for dk in range(nk)
        if dl or dh or dk
    ]
    z_partners = [
        {**step("vir_1", l, dl, nl), **step("ph", h, dh, nh), **step("vec", k, dk, nk)}
        for dl, dh, dk in z_steps
    ]
    z_hops = [nl * min(dh, nh - dh) + dl for dl, dh, dk in z_steps]

    loads = []

    def load(whole, *copies):
        sem = load_sem.at[len(loads)]
        for src, dst in copies:
            pltpu.make_async_copy(src, dst, sem).start()
        loads.append(pltpu.make_async_copy(whole, whole, sem))
        return loads[-1]

    def slab_copy(s):
        return factor.at[:, :, pl.ds(s * slab, slab)], factor_raw.at[s]

    first_load = load(factor_raw.at[0], slab_copy(0))
    block_loads = [
        load(owner_s, (owner_of, owner_s)),
        load(slot_s, (slot_of, slot_s)),
        load(cyc_v, (cycle_amp, cyc_v)),
    ]

    barrier = pltpu.get_barrier_semaphore()
    partners = list(zip(z_hops, z_partners))
    for dx, dy in zip(x_steps, y_steps):
        for dl in reversed(range(nl)):
            far_x, far_y = min(dx, nx - dx) + dl, min(dy, ny - dy) + dl
            partners.append((far_x, {**step("vir_0", x, dx, nx), **step("vir_1", l, dl, nl)}))
            partners.append((far_y, {**step("vir_2", y, dy, ny), **step("vir_1", l, dl, nl)}))
    for _, moved in sorted(partners, key=lambda partner: -partner[0]):
        pl.semaphore_signal(
            barrier, inc=1, device_id=at(**moved), device_id_type=pl.DeviceIdType.MESH
        )

    slots_load = load(slots_v, (ov_slots, slots_v))
    factor_load = load(factor_raw.at[1:], *[slab_copy(s) for s in range(1, nx)])
    amp_load = load(
        amp_raw,
        *[
            (amp.at[pl.ds(s * slab, slab)], amp_raw.at[pl.ds(s * slab, slab)])
            for s in range(nx)
        ],
    )
    late_loads = [
        load(pairs_v, (ov_pairs, pairs_v)),
        load(eps_vir_s, (eps_vir, eps_vir_s)),
        load(eps_occ_s, (eps_occ, eps_occ_s)),
    ]

    first_load.wait()
    first = factor_raw[0].astype(F32)[:, :, :1]
    lane_of = lax.broadcasted_iota(jnp.int32, (pc, R, pc), 2)
    row_of = lax.broadcasted_iota(jnp.int32, (pc, R, pc), 0)
    piece = jnp.sum(jnp.where(lane_of == row_of, first, 0.0), axis=0).astype(BF16)
    outer = jnp.where(l == 0, y, x)
    inner = jnp.where(l == 0, x, y)
    rows[l, outer, inner] = piece

    for copy in block_loads:
        copy.wait()
    blocks = [jnp.concatenate([cyc_v[n].astype(F32)] * 2, axis=1) for n in range(2)]
    lane_half = (
        lax.broadcasted_iota(jnp.int32, blocks[0].shape, 1) >= blocks[0].shape[1] // 2
    ).astype(jnp.int32)
    for target in range(nh):
        for pair in range(2):
            total = jnp.zeros_like(blocks[0])
            for n in range(2):
                wanted = jnp.where(owner_s[n] == target, slot_s[n], -1)
                total = total + jnp.where(lane_half + 2 * pair == wanted, blocks[n], 0.0)
            blk_send[target, pair] = total.astype(BF16)

    pl.semaphore_wait(barrier, len(partners))

    pick = rows.at[l, outer, inner]
    copies = []
    for d in far_first(nx) + [0]:
        for dl in reversed(range(nl)):
            if d or dl:
                moved = {
                    "vir_0": lax.rem(x + d * (1 - l), nx),
                    "vir_2": lax.rem(y + d * l, ny),
                    **step("vir_1", l, dl, nl),
                }
                copies.append((pick, pick, moved))
    gather1 = exchange(copies)
    owners = []
    for d in far_first(nh):
        moved = step("ph", h, d, nh)
        owners.append((blk_send.at[moved["ph"]], blk_recv.at[d - 1], moved))
    to_owner = exchange(owners)

    amp_load.wait()

    def split_amp(s, carry):
        for u in range(2):
            chunk = amp_raw[pl.ds(pl.multiple_of((2 * s + u) * slab, slab), slab)].astype(F32)
            for n in range(pairs // LANES):
                amp_wide[u, n] = chunk[:, :, n * LANES : (n + 1) * LANES].reshape(slab * R, LANES)
        for d in range(R):
            for n in range(pairs // LANES):
                columns = slice(n * LANES, (n + 1) * LANES)
                for t in range(ny):
                    both = [amp_wide[u, n, pl.ds(t * R * R + d, R, stride=R), :] for u in range(2)]
                    place = slot_at(lax.rem(t - y + ny, ny), ny)
                    amp_d[d, place, pl.ds(pl.multiple_of(s * 2 * R, 2 * R), 2 * R), columns] = (
                        jnp.concatenate(both, axis=0).astype(BF16)
                    )
                for u in range(2):
                    place = slot_at(lax.rem(2 * s + u - x + nx, nx), nx)
                    amp_d[d, place, part_rows:, columns] = amp_wide[
                        u, n, pl.ds(part_rows * R + d, part_rows, stride=R), :
                    ].astype(BF16)
        return carry

    lax.fori_loop(0, nx // 2, split_amp, 0)

    order_x, order_y = slot_order(nx), slot_order(ny)
    groups = [(0, nx // 2), (nx // 2, nx * 3 // 4), (nx * 3 // 4, nx)] if nx > 2 else [(0, 2)]

    gather1.wait_recv()
    gather2 = []
    for low_slot, high_slot in reversed(groups):
        copies = []
        for dx, dy in zip(x_steps, y_steps):
            own0, own1 = rows.at[0, y], rows.at[1, x]
            if low_slot <= order_y.index(ny - dy) < high_slot:
                copies.append((own0, own0, step("vir_2", y, dy, ny)))
                copies.append((own1, own1, step("vir_0", x, dx, nx)))
        gather2.insert(0, exchange(copies))

    slots_load.wait()
    to_owner.wait_recv()
    arranged = blk_send[h].astype(F32)
    for d in range(nh - 1):
        arranged = arranged + blk_recv[d].astype(F32)
    arranged = arranged.astype(BF16)
    depth = slots_v.shape[0] // 2
    for q in range(nh * nk):
        chunk = slice(q * pc, (q + 1) * pc)
        part[q] = (
            jnp.dot(arranged[0], slots_v[:depth, chunk], preferred_element_type=F32)
            + jnp.dot(arranged[1], slots_v[depth:, chunk], preferred_element_type=F32)
        ).astype(BF16)
    copies = []
    for n, moved in enumerate(z_partners):
        copies.append((part.at[moved["ph"] * nk + moved["vec"]], part_recv.at[n], moved))
    to_chunk = exchange(copies)

    factor_load.wait()

    def turn_factor(s, carry):
        factor_wide[...] = factor_raw[s].astype(F32).reshape(factor_wide.shape)
        base = pl.multiple_of(s * part_rows, part_rows)
        for d in range(R):
            turned = factor_wide[pl.ds(d, pc, stride=R), :].T.astype(BF16)
            for c in range(nl):
                factor_t[c, pl.ds(base, part_rows), d * pc : (d + 1) * pc] = turned[
                    c * part_rows : (c + 1) * part_rows
                ]
        return carry

    lax.fori_loop(0, nx, turn_factor, 0)

    mid = c1.shape[1]
    for index, (low_slot, high_slot) in enumerate(groups):
        gather2[index].wait_recv()
        for s in range(low_slot, high_slot):
            low = rows[0, lax.rem(y + order_y[s], ny)].astype(F32).reshape(part_rows, pc)
            high = rows[1, lax.rem(x + order_x[s], nx)].astype(F32).reshape(part_rows, pc)
            row_lhs[:, s * slab : (s + 1) * slab] = (
                jnp.concatenate([low, high], axis=0).T.astype(BF16)
            )

        def make_half(d, carry):
            lines = pl.ds(pl.multiple_of(d * pc, pc), pc)
            depth = (high_slot - low_slot) * slab
            value = jnp.dot(
                row_lhs[:, low_slot * slab : high_slot * slab],
                amp_d[d, low_slot:high_slot].reshape(depth, pairs),
                preferred_element_type=F32,
            )
            if index:
                value = half_sum[lines, :] + value
            if index == len(groups) - 1:
                half[lines, :] = value.astype(BF16)
            else:
                half_sum[lines, :] = value
            return carry

        lax.fori_loop(0, R, make_half, 0, unroll=True)

    swap = []
    for c in range(nl):
        full = jnp.dot(factor_t[c], half[...], preferred_element_type=F32)
        for n in range(nk):
            grid[c, n] = full[:, n * LANES : (n + 1) * LANES].reshape(nx, ny, R, LANES)
            grid_send[c, n] = grid[c, n].astype(BF16)
        swap.append(
            exchange([(grid_send.at[c, 1 - k], grid_recv.at[c], step("vec", k, 1, nk))])
        )

    to_chunk.wait_recv()
    total = part[h * nk + k].astype(F32)
    for n in range(len(z_partners)):
        total = total + part_recv[n].astype(F32)
    parts = [total[:mid], total[mid:]]
    c1[0], c1[1] = [p.astype(BF16) for p in parts]
    copies = []
    for dx, dy in zip(x_steps, y_steps):
        copies.append((c1.at[0], c1_recv.at[0, dx - 1], step("vir_0", x, dx, nx)))
        copies.append((c1.at[1], c1_recv.at[1, dy - 1], step("vir_2", y, dy, ny)))
    sum1 = exchange(copies)

    scatter1 = []
    for c in range(nl):
        swap[c].wait_recv()
        wide[c] = grid[c, k] + grid_recv[c].astype(F32)
        if c == 0:
            stage[0] = wide[0].astype(BF16)
        else:
            for s in range(nx):
                for t in range(ny):
                    stage[1, t, s] = wide[1, s, t].astype(BF16)
        copies = []
        for d in x_steps if c == 0 else y_steps:
            moved = step("vir_0", x, d, nx) if c == 0 else step("vir_2", y, d, ny)
            there = moved["vir_0"] if c == 0 else moved["vir_2"]
            copies.append((stage.at[c, there], stage_recv.at[c, d - 1], moved))
        scatter1.append(exchange(copies))

    sum1.wait_recv()
    for c in range(2):
        for d in range(nx - 1):
            parts[c] = parts[c] + c1_recv[c, d].astype(F32)
        c2[c] = parts[c].astype(BF16)
    copies = []
    for dx, dy in zip(x_steps, y_steps):
        copies.append((c2.at[0], c2_recv.at[0, dy - 1], step("vir_2", y, dy, ny)))
        copies.append((c2.at[1], c2_recv.at[1, dx - 1], step("vir_0", x, dx, nx)))
    sum2 = exchange(copies)

    scatter2 = []
    for c in range(nl):
        scatter1[c].wait_recv()
        total = wide[0, x] if c == 0 else wide[1, :, y]
        for d in range(nx - 1):
            total = total + stage_recv[c, d].astype(F32)
        second[c] = total
        copies = []
        for d in y_steps if c == 0 else x_steps:
            moved = step("vir_2", y, d, ny) if c == 0 else step("vir_0", x, d, nx)
            there = moved["vir_2"] if c == 0 else moved["vir_0"]
            copies.append((second.at[c, there], second_recv.at[c, d - 1], moved))
        scatter2.append(exchange(copies))

    sum2.wait_recv()
    both = []
    for c in range(2):
        total = parts[c]
        for d in range(nx - 1):
            total = total + c2_recv[c, d].astype(F32)
        both.append(total)
    coupling = jnp.concatenate(both, axis=0)
    occ = coupling.shape[0]
    spread = jnp.broadcast_to(coupling[:, None, :], (occ, R, pc)).reshape(occ * R, pc)
    for copy in late_loads:
        copy.wait()
    second_count = ov_pairs.shape[0]
    ov = pairs_v[...].astype(F32).reshape(second_count * R, pc).astype(BF16)
    every = lax.dot_general(
        ov, spread.astype(BF16), (((1,), (1,)), ((), ())), preferred_element_type=F32
    )
    lane_j = lax.rem(lax.broadcasted_iota(jnp.int32, (R, pairs), 1), second_count)
    term = jnp.zeros((R, pairs), F32)
    for j in range(second_count):
        term = term + jnp.where(lane_j == j, every[j * R : (j + 1) * R], 0.0)
    for n in range(nk):
        cyc[n] = term[:, n * LANES : (n + 1) * LANES]
    per_half = LANES // out_ref.shape[2]
    copies = []
    for (dl, dh, dk), moved in zip(z_steps, z_partners):
        if dl == 0:
            there = moved["ph"] * nk + moved["vec"]
            copies.append((cyc.at[there // per_half], cyc_recv.at[len(copies)], moved))
    to_pairs = exchange(copies)

    width = out_ref.shape[2]
    q = h * nk + k
    line = lax.broadcasted_iota(jnp.int32, (R, width), 0)
    lane = lax.broadcasted_iota(jnp.int32, (R, width), 1)
    slab_start = ((x * nl + l) * ny + y) * R
    virtual = jnp.zeros((R, width), F32)
    for r in range(R):
        virtual = jnp.where(line == r, eps_vir_s[slab_start + r], virtual)
    first_occ = jnp.zeros((R, width), F32)
    for n in range(width // second_count):
        first_occ = jnp.where(
            lane // second_count == n, eps_occ_s[q * (width // second_count) + n], first_occ
        )
    second_occ = jnp.zeros((R, width), F32)
    for n in range(second_count):
        second_occ = jnp.where(lax.rem(lane, second_count) == n, eps_occ_s[n], second_occ)
    denominator = (eps_vir_s[0] + virtual) - first_occ - second_occ

    for c in range(nl):
        scatter2[c].wait_recv()
        total = second[0, y] if c == 0 else second[1, x]
        for d in range(nx - 1):
            total = total + second_recv[c, d]
        third[c] = total

    last = next(ids)
    mine = h * nl + l
    own_source = q // per_half == k
    for m in range(per_half):
        for c in range(nl):
            there = k * per_half + m
            th, tk = there // nk, lax.rem(there, nk)
            away = jnp.logical_not((th == h) & (tk == k) & (c == l))
            copy = pltpu.make_async_remote_copy(
                src_ref=third.at[c],
                dst_ref=third_recv.at[mine],
                send_sem=send_sem.at[1],
                recv_sem=recv_sem.at[last],
                device_id=at(ph=th, vec=tk, vir_1=jnp.int32(c)),
                device_id_type=pl.DeviceIdType.MESH,
            )
            pl.when(away)(copy.start)

    @pl.when(own_source)
    def _():
        third_recv[mine] = third[l]

    def finals(count):
        whole = third_recv.at[pl.ds(0, count)]
        return pltpu.make_async_remote_copy(
            src_ref=whole,
            dst_ref=whole,
            send_sem=send_sem.at[1],
            recv_sem=recv_sem.at[last],
            device_id=at(**step("vir_1", l, 1, nl)),
            device_id_type=pl.DeviceIdType.MESH,
        )

    others = per_half * nl

    to_pairs.wait_recv()
    cycle_sum = cyc[q // per_half]
    for n in range(nh * nk - 1):
        cycle_sum = cycle_sum + cyc_recv[n]
    whole = tally.at[pl.ds(0, sum(sent_units))]
    remote(whole, whole, at(**step("vec", k, 1, nk)), 0).wait_send()
    pl.when(own_source)(finals(others - 1).wait_recv)
    pl.when(jnp.logical_not(own_source))(finals(others).wait_recv)

    total = cycle_sum
    for s in range(nh * nl):
        total = total + third_recv[s]
    mine_lanes = lax.rem(q, per_half)
    result = jnp.zeros((R, width), F32)
    for m in range(per_half):
        result = jnp.where(mine_lanes == m, total[:, m * width : (m + 1) * width], result)
    out_ref[0] = result.astype(BF16).astype(F32)
    out_ref[1] = denominator
    pl.when(own_source)(finals(others - 1).wait_send)
    pl.when(jnp.logical_not(own_source))(finals(others).wait_send)


def local(
    sizes,
    vv_factor,
    ladder_amp,
    cycle_amp,
    ov_slots,
    owner_of,
    slot_of,
    ov_pairs,
    eps_vir,
    eps_occ,
):
    nx, nl, ny, nh, nk = sizes
    pc, _, virtuals = vv_factor.shape
    pairs = ladder_amp.shape[2]
    capacity, chol, part_w = ov_slots.shape
    occ = cycle_amp.shape[1]
    second_count = ov_pairs.shape[1]
    slots_t = jnp.transpose(ov_slots, (0, 2, 1)).reshape(capacity * part_w, chol)
    pairs_t = jnp.transpose(ov_pairs, (1, 2, 0))
    slab = nl * ny * R
    width = pairs // (nh * nk)
    steps = nx - 1
    VM = pltpu.VMEM
    scratch = [
        pltpu.SMEM(owner_of.shape, jnp.int32),
        pltpu.SMEM(slot_of.shape, jnp.int32),
        pltpu.SMEM(eps_vir.shape, F32),
        pltpu.SMEM(eps_occ.shape, F32),
        VM((nx, pc, R, slab), BF16),
        VM((pc * R, slab), F32),
        VM((nl, nx * ny * R, R * pc), BF16),
        VM(ladder_amp.shape, BF16),
        VM((2, pairs // LANES, slab * R, LANES), F32),
        VM((R, nx, slab, pairs), BF16),
        VM((nl, nx, ny, R, pc), BF16),
        VM((pc, virtuals), BF16),
        VM((R * pc, pairs), F32),
        VM((R * pc, pairs), BF16),
        VM(slots_t.shape, BF16),
        VM(cycle_amp.shape, BF16),
        VM(pairs_t.shape, BF16),
        VM((nh, 2, occ, 2 * part_w), BF16),
        VM((nh - 1, 2, occ, 2 * part_w), BF16),
        VM((nh * nk, occ, pc), BF16),
        VM((nh * nk * nl - 1, occ, pc), BF16),
        VM((2, occ // 2, pc), BF16),
        VM((2, steps, occ // 2, pc), BF16),
        VM((2, occ // 2, pc), BF16),
        VM((2, steps, occ // 2, pc), BF16),
        VM((nk, R, LANES), F32),
        VM((nh * nk - 1, R, LANES), F32),
        VM((nl, nk, nx, ny, R, LANES), F32),
        VM((nl, nk, nx, ny, R, LANES), BF16),
        VM((nl, nx, ny, R, LANES), BF16),
        VM((nl, nx, ny, R, LANES), F32),
        VM((nl, nx, ny, R, LANES), BF16),
        VM((nl, steps, ny, R, LANES), BF16),
        VM((nl, ny, R, LANES), F32),
        VM((nl, steps, R, LANES), F32),
        VM((nl, R, LANES), F32),
        VM((nh * nl, R, LANES), F32),
        VM((1024, R, pc), BF16),
        pltpu.SemaphoreType.DMA((10,)),
        pltpu.SemaphoreType.DMA((2,)),
        pltpu.SemaphoreType.DMA((16,)),
    ]
    hbm = pl.BlockSpec(memory_space=pltpu.MemorySpace.HBM)
    out = pl.pallas_call(
        functools.partial(body, sizes),
        out_shape=pltpu.VMEM((2, R, width), F32),
        in_specs=[hbm] * 9,
        out_specs=pl.BlockSpec(memory_space=pltpu.VMEM),
        scratch_shapes=scratch,
        compiler_params=pltpu.CompilerParams(
            collective_id=0, has_side_effects=True, vmem_limit_bytes=63 * 1024 * 1024
        ),
    )(
        vv_factor,
        ladder_amp,
        cycle_amp,
        slots_t,
        owner_of,
        slot_of,
        pairs_t,
        eps_vir,
        eps_occ,
    )
    residual = out[0].astype(BF16)
    return residual, residual.astype(F32) / out[1]


def build(devices, sizes):
    torus = Mesh(devices.reshape(sizes), AXES)
    placed = (
        P(("ph", "vec"), VIR, None),
        P(None, VIR, None),
        P(VIR_PH, None, "vec"),
        P(VIR_PH, None, "vec"),
        P(VIR_PH),
        P(VIR_PH),
        P(("ph", "vec"), None, VIR),
        P(),
        P(),
    )
    return jax.shard_map(
        functools.partial(local, sizes),
        mesh=torus,
        in_specs=placed,
        out_specs=(P(VIR, ("ph", "vec")), P(VIR, ("ph", "vec"))),
        check_vma=False,
    )


def solution(mesh):
    return build(mesh.devices, (8, 2, 8, mesh.shape["ph"], mesh.shape["vec"]))
```
